1024 devices in a mesh: row: 16 (over z_hi, y), col: 16 (over z_lo, core), depth: 4 (over x).
Axes of the slice: x: 4, y: 4, z: 32 (z_hi: 4, z_lo: 8; z = z_hi * 8 + z_lo), core: 2. Of those that a mesh axis runs over, the one named last changes fastest.
Arguments:
- gate_pre: bfloat16 [2048, 26624], P(('col', 'depth'), 'row'), may hold values from -6 to 6
- up_pre: bfloat16 [2048, 26624], P(('col', 'depth'), 'row'), may hold values from -6 to 6
- out_grad: bfloat16 [2048, 16384], P(('row', 'depth'), 'col'), may hold values from -2 to 2
- down_weight: bfloat16 [26624, 16384], P('row', 'col'), may hold values from -0.0390625 to 0.0390625
Outputs:
- weight_grad: bfloat16 [26624, 16384], P(('row', 'depth'), 'col')
- gate_grad: bfloat16 [2048, 26624], P(('col', 'depth'), 'row')
- up_grad: bfloat16 [2048, 26624], P(('col', 'depth'), 'row')
The draws below stay inside these ranges and needn't reach their ends.
All inputs are finite; a program needn't handle non-finite values.
Results may differ from the reference program's by a relative error of at most 0.009.
Values may be sent and summed in bfloat16 or wider, within the bound.
A program may use at most 64 MiB of HBM per device.

```python
import jax
import jax.numpy as jnp
from jax import lax

D = 16384
FF = 26624
TOK_DEV = 32
TOKENS = 2048
N_ROW = 16
N_DEPTH = 4


def steps_of(stream_key, dims, pieces, smallest, largest):
    def one(axis_at, shards_of):
        draws = jax.random.uniform(jax.random.fold_in(jax.random.fold_in(stream_key, 6), axis_at), (shards_of,), jnp.float32, smallest / len(pieces), largest / len(pieces))
        return jnp.repeat(jnp.exp(draws), dims[axis_at] // shards_of).reshape((-1,) + (1,) * (len(dims) - axis_at - 1))

    loudness = one(*pieces[0])
    for cut in pieces[1:]:
        loudness = loudness * one(*cut)
    return loudness


def centred(own_key, extent, spread, bound, pieces=(), held_as=jnp.bfloat16):
    entries = spread * jax.random.normal(own_key, extent, jnp.float32)
    if pieces:
        entries = entries * steps_of(own_key, extent, pieces, -0.22, 0.18)
    return jnp.clip(entries, -bound, bound).astype(held_as)


def setup_inputs(seed: int = 0) -> dict:
    arg_keys = jax.random.split(jax.random.key(seed), 5)
    return {
        "gate_pre": centred(arg_keys[0], (TOKENS, FF), 1.5, 6.0, ((0, 64), (1, 16))),
        "up_pre": centred(arg_keys[1], (TOKENS, FF), 1.0, 6.0, ((0, 64), (1, 16))),
        "out_grad": centred(arg_keys[2], (TOKENS, D), (TOKENS ** -0.25), 2.0, ((0, 64), (1, 16))),
        "down_weight": centred(arg_keys[3], (FF, D), FF ** -0.5, 0.0390625, ((0, 16), (1, 16))),
    }


def reference(gate_pre, up_pre, out_grad, down_weight):
    gate_vals = gate_pre.astype(jnp.float32)
    up_vals = up_pre.astype(jnp.float32)
    sigma_gate = jax.nn.sigmoid(gate_vals)
    act = gate_vals * sigma_gate
    hidden = (act * up_vals).astype(jnp.bfloat16)
    hidden_grad = lax.dot_general(out_grad, down_weight, (((1,), (1,)), ((), ())), preferred_element_type=jnp.float32)
    up_grad = (hidden_grad * act).astype(jnp.bfloat16)
    gate_grad = (hidden_grad * up_vals * sigma_gate * (1.0 + gate_vals * (1.0 - sigma_gate))).astype(jnp.bfloat16)
    hidden_blocks = hidden.reshape(N_ROW, N_DEPTH, TOK_DEV, FF)
    grad_blocks = out_grad.reshape(N_ROW, N_DEPTH, TOK_DEV, D)

    def add_layer(total, layer):
        rows_hidden = lax.dynamic_index_in_dim(hidden_blocks, layer, 1, keepdims=False).reshape(N_ROW * TOK_DEV, FF)
        rows_grad = lax.dynamic_index_in_dim(grad_blocks, layer, 1, keepdims=False).reshape(N_ROW * TOK_DEV, D)
        partial_sum = lax.dot_general(rows_hidden, rows_grad, (((0,), (0,)), ((), ())), preferred_element_type=jnp.float32)
        rounded = lax.optimization_barrier(partial_sum.astype(jnp.bfloat16))
        return total + rounded.astype(jnp.float32), None

    total, unused = lax.scan(add_layer, jnp.zeros((FF, D), jnp.float32), jnp.arange(N_DEPTH, dtype=jnp.int32))
    weight_grad = total.astype(jnp.bfloat16)
    return weight_grad, gate_grad, up_grad
```

```python
import functools

import jax
import jax.numpy as jnp
from jax import lax
from jax.experimental import pallas as pl
from jax.experimental.pallas import tpu as pltpu
from jax.sharding import Mesh
from jax.sharding import PartitionSpec as P

MESH = pl.DeviceIdType.MESH
COL = ("zl", "core")
ROW = ("zh", "y")
F32 = jnp.float32
BF16 = jnp.bfloat16
NT = (((1,), (1,)), ((), ()))


def kernel(
    gate_ref, up_ref, og_ref, w_ref,
    dw_ref, gg_ref, ug_ref,
    G, W, gv, uv, act, fac, HS, HX, HT, PF, PB, PR, RB, SB, HG, ACC,
    lsem, zs, zr, ys, yr, xs, xr, hs, hr, brs, brr, bls, blr, bps, bpr, ps, pr, cs, cr,
):
    zo, y, k, c, x = (lax.axis_index(a) for a in ("zh", "y", "zl", "core", "x"))
    zp, zm = lax.rem(zo + 1, 4), lax.rem(zo + 3, 4)
    yp, ym = lax.rem(y + 1, 4), lax.rem(y + 3, 4)
    xp, xm = lax.rem(x + 1, 4), lax.rem(x + 3, 4)
    sends = []

    def copy(src, dst, ss, rs, dev):
        return pltpu.make_async_remote_copy(
            src_ref=src, dst_ref=dst, send_sem=ss, recv_sem=rs, device_id=dev, device_id_type=MESH
        )

    def send(*args):
        cp = copy(*args)
        cp.start()
        sends.append(cp)

    loads = [
        pltpu.make_async_copy(og_ref, G.at[zo, y, x], lsem.at[0]),
        pltpu.make_async_copy(gate_ref, gv, lsem.at[1]),
        pltpu.make_async_copy(up_ref, uv, lsem.at[2]),
        pltpu.make_async_copy(w_ref, W, lsem.at[3]),
    ]
    for cp in loads:
        cp.start()
    barrier = pltpu.get_barrier_semaphore()
    peers = [{"zh": zp}, {"zh": zm}, {"y": yp}, {"y": ym}, {"x": xp}, {"x": xm},
             {"x": lax.rem(x + 2, 4)}, {"core": 1 - c}, {"zl": lax.rem(k + 1, 8)}, {"zl": lax.rem(k + 7, 8)}]
    for dev in peers:
        pl.semaphore_signal(barrier, inc=1, device_id=dev, device_id_type=MESH)

    loads[1].wait()
    loads[2].wait()
    g = gv[...].astype(F32)
    u = uv[...].astype(F32)
    sig = jax.nn.sigmoid(g)
    a = g * sig
    act[...] = a
    fac[...] = u * sig * (1.0 + g * (1.0 - sig))
    h = a * u
    for s in range(4):
        rolled = h if s == 0 else pltpu.roll(h, 1664 - 416 * s, 1)
        HS[s] = rolled[:, :512].astype(BF16)
    loads[0].wait()

    pl.semaphore_wait(barrier, len(peers))

    def half(i):
        return pl.ds(16 * i, 16)

    def z_first():
        own = G.at[zo, y, x]
        for i, (hp, hm) in enumerate(((0, 1), (1, 0))):
            send(own.at[half(hp)], own.at[half(hp)], zs.at[0, i], zr.at[0, i], {"zh": zp})
            send(own.at[half(hm)], own.at[half(hm)], zs.at[1, i], zr.at[1, i], {"zh": zm})

    def z_wait(d, i):
        zh = (zm, zp)[d] if i < 2 else lax.rem(zo + 2, 4)
        hh = d if i != 1 else 1 - d
        dst = G.at[zh, y, x].at[half(hh)]
        copy(dst, dst, zs.at[d, i], zr.at[d, i], {"zh": zp}).wait_recv()

    def z_relay():
        z_wait(0, 0)
        r = G.at[zm, y, x].at[half(0)]
        send(r, r, zs.at[0, 2], zr.at[0, 2], {"zh": zp})
        z_wait(1, 0)
        r = G.at[zp, y, x].at[half(1)]
        send(r, r, zs.at[1, 2], zr.at[1, 2], {"zh": zm})
        z_wait(0, 1)
        z_wait(1, 1)

    def y_first(q):
        b = G.at[lax.rem(zo + q, 4), y, x]
        send(b, b, ys.at[q, 0], yr.at[q, 0], {"y": yp})
        send(b, b, ys.at[q, 1], yr.at[q, 1], {"y": ym})

    def y_relay(q):
        zh = lax.rem(zo + q, 4)
        b = G.at[zh, ym, x]
        copy(b, b, ys.at[q, 0], yr.at[q, 0], {"y": yp}).wait_recv()
        b = b.at[half(0)]
        send(b, b, ys.at[q, 2], yr.at[q, 2], {"y": yp})
        b = G.at[zh, yp, x]
        copy(b, b, ys.at[q, 1], yr.at[q, 1], {"y": yp}).wait_recv()
        b = b.at[half(1)]
        send(b, b, ys.at[q, 3], yr.at[q, 3], {"y": ym})

    def y_last(q):
        b = G.at[lax.rem(zo + q, 4), lax.rem(y + 2, 4), x]
        for i in range(2):
            d = b.at[half(i)]
            copy(d, d, ys.at[q, 2 + i], yr.at[q, 2 + i], {"y": yp}).wait_recv()

    def x_first(q):
        b = G.at[lax.rem(zo + q, 4), :, x]
        send(b, b, xs.at[q, 0], xr.at[q, 0], {"x": xp})
        send(b, b, xs.at[q, 1], xr.at[q, 1], {"x": xm})

    def x_relay(q):
        zh = lax.rem(zo + q, 4)
        b = G.at[zh, :, xm]
        copy(b, b, xs.at[q, 0], xr.at[q, 0], {"x": xp}).wait_recv()
        b = G.at[zh, pl.ds(0, 2), xm]
        send(b, b, xs.at[q, 2], xr.at[q, 2], {"x": xp})
        b = G.at[zh, :, xp]
        copy(b, b, xs.at[q, 1], xr.at[q, 1], {"x": xp}).wait_recv()
        b = G.at[zh, pl.ds(2, 2), xp]
        send(b, b, xs.at[q, 3], xr.at[q, 3], {"x": xm})

    def x_last(q):
        zh = lax.rem(zo + q, 4)
        for i in range(2):
            d = G.at[zh, pl.ds(2 * i, 2), lax.rem(x + 2, 4)]
            copy(d, d, xs.at[q, 2 + i], xr.at[q, 2 + i], {"x": xp}).wait_recv()

    def h_first():
        for o in range(1, 4):
            to = lax.rem(x + o, 4)
            send(HS.at[to], HX.at[x], hs.at[o - 1], hr.at[o - 1], {"x": to})
        HX[x] = HS[x]

    def h_last():
        for o in range(1, 4):
            d = HX.at[lax.rem(x + 4 - o, 4)]
            copy(d, d, hs.at[o - 1], hr.at[o - 1], {"x": xp}).wait_recv()
        t = HX[...].astype(F32).reshape(128, 512).T
        HT[2 * k + c] = t[:416].astype(BF16)

    def ht(o, i):
        return HT.at[2 * o + c, pl.ds(208 * i, 208)]

    def right(o, i, idx):
        b = ht(o, i)
        return copy(b, b, brs.at[idx], brr.at[idx], {"zl": k + 1})

    def left(o, i, idx):
        b = ht(o, i)
        return copy(b, b, bls.at[idx], blr.at[idx], {"zl": k - 1})

    def across(o):
        return copy(HT.at[2 * o + c], HT.at[2 * o + c], bps.at[o], bpr.at[o], {"core": 1 - c})

    def b_first():
        for i in range(2):
            @pl.when(k < 7)
            def _():
                right(k, i, i).start()

            @pl.when(k > 0)
            def _():
                left(k, i, i).start()
        across(k).start()

    def b_steps(lo, hi):
        def step(s, carry):
            for i in range(2):
                @pl.when(k - 1 - s >= 0)
                def _():
                    o = k - 1 - s
                    right(o, i, 2 * s + i).wait_recv()

                    @pl.when(k < 7)
                    def _():
                        right(o, i, 2 * s + 2 + i).start()

                @pl.when(k + 1 + s <= 7)
                def _():
                    o = k + 1 + s
                    left(o, i, 2 * s + i).wait_recv()

                    @pl.when(k > 0)
                    def _():
                        left(o, i, 2 * s + 2 + i).start()

            @pl.when(k - 1 - s >= 0)
            def _():
                across(k - 1 - s).start()

            @pl.when(k + 1 + s <= 7)
            def _():
                across(k + 1 + s).start()

            return carry

        lax.fori_loop(lo, hi, step, 0)

    def b_last():
        def step(o, carry):
            d = HT.at[2 * o + 1 - c]
            copy(d, d, bps.at[o], bpr.at[o], {"core": 1 - c}).wait_recv()
            return carry

        lax.fori_loop(0, 8, step, 0)

    def terms(q):
        zh = lax.rem(zo + q, 4)
        rows = G[zh, :, x].reshape(128, 1024)

        def part(n0, nn):
            res = lax.dot_general(rows, W[pl.ds(n0, nn), :], NT, preferred_element_type=F32)
            res = res.reshape(2, 2, 32, nn)
            PF[pl.ds(2 * zh, 2), :, :, pl.ds(n0, nn)] = res
            PB[pl.ds(2 * zh, 2), :, :, pl.ds(n0, nn)] = res.astype(BF16)

        def step(i, carry):
            part(pl.multiple_of(i * 256, 256), 256)
            return carry

        lax.fori_loop(0, 6, step, 0)
        part(1536, 128)
        send(PB.at[pl.ds(2 * zh, 2), 1 - c], PR.at[pl.ds(2 * zh, 2)], ps.at[q], pr.at[q], {"core": 1 - c})

    def terms_last(q):
        zh = lax.rem(zo + q, 4)
        d = PR.at[pl.ds(2 * zh, 2)]
        copy(d, d, ps.at[q], pr.at[q], {"core": 1 - c}).wait_recv()

    def c_copy(way, d, i, dev):
        return copy(SB.at[d, half(i)], RB.at[way, d, half(i)], cs.at[d, i], cr.at[way, d, i], dev)

    def c_steps(lo, hi):
        def one(way, pos, d, i, to):
            mine = PF[d, c, half(i)] + PR[d, half(i)].astype(F32)

            @pl.when(pos == 0)
            def _():
                SB[d, half(i)] = mine.astype(BF16)

            @pl.when(pos > 0)
            def _():
                c_copy(way, d, i, {"zl": to}).wait_recv()
                SB[d, half(i)] = (mine + RB[way, d, half(i)].astype(F32)).astype(BF16)

            c_copy(way, d, i, {"zl": to}).start()

        def step(t, carry):
            for i in range(2):
                q = t - k - i
                j = q // 2

                @pl.when((q >= 0) & (lax.rem(q + 16, 2) == 0) & (7 - j > k))
                def _():
                    one(0, k, 7 - j, i, k + 1)

                r = t - (7 - k) - i
                m = r // 2

                @pl.when((r >= 0) & (lax.rem(r + 16, 2) == 0) & (m < k))
                def _():
                    one(1, 7 - k, m, i, k - 1)

            return carry

        lax.fori_loop(lo, hi, step, 0)

    def c_last():
        HG[...] = PF[k, c] + PR[k].astype(F32)

        @pl.when(k > 0)
        def _():
            for i in range(2):
                c_copy(0, k, i, {"zl": k - 1}).wait_recv()
            HG[...] += RB[0, k].astype(F32)

        @pl.when(k < 7)
        def _():
            for i in range(2):
                c_copy(1, k, i, {"zl": k + 1}).wait_recv()
            HG[...] += RB[1, k].astype(F32)

        hg = HG[...]
        ug_ref[...] = (hg * act[...]).astype(BF16)
        gg_ref[...] = (hg * fac[...]).astype(BF16)

    def dw(q, first=False):
        zh = lax.rem(zo + q, 4)
        lhs = jnp.concatenate([HT[4 * zh + i] for i in range(4)], axis=1)

        def step(n, carry):
            cols = pl.ds(pl.multiple_of(n * 256, 256), 256)
            rhs = G[zh, :, :, :, cols].reshape(512, 256)
            res = jnp.dot(lhs, rhs, preferred_element_type=F32)
            ACC[:, cols] = res if first else ACC[:, cols] + res
            return carry

        lax.fori_loop(0, 4, step, 0)

    z_first()
    y_first(0)
    h_first()
    h_last()
    b_first()
    y_relay(0)
    y_last(0)
    x_first(0)
    loads[3].wait()
    terms(0)
    b_steps(0, 2)
    z_relay()
    y_first(1)
    y_first(3)
    b_steps(2, 3)
    y_relay(1)
    y_relay(3)
    x_relay(0)
    y_last(1)
    y_last(3)
    x_first(1)
    x_first(3)
    terms(1)
    terms(3)
    b_steps(3, 4)
    z_wait(0, 2)
    z_wait(1, 2)
    y_first(2)
    b_steps(4, 5)
    y_relay(2)
    y_last(2)
    x_first(2)
    terms(2)
    b_steps(5, 7)
    for q in range(4):
        terms_last(q)
    x_relay(1)
    x_relay(3)
    c_steps(0, 4)
    b_last()
    x_last(0)
    dw(0, True)
    c_steps(4, 7)
    x_relay(2)
    x_last(1)
    dw(1)
    c_steps(7, 10)
    x_last(3)
    dw(3)
    c_steps(10, 14)
    x_last(2)
    dw(2)
    dw_ref[...] = ACC[...].astype(BF16)
    c_last()

    for cp in sends:
        cp.wait_send()

    def drain_b(s, carry):
        for i in range(2):
            @pl.when((k - s >= 0) & (k < 7))
            def _():
                right(k - s, i, 2 * s + i).wait_send()

            @pl.when((k + s <= 7) & (k > 0))
            def _():
                left(k + s, i, 2 * s + i).wait_send()

        across(s).wait_send()
        return carry

    lax.fori_loop(0, 8, drain_b, 0)

    def drain_c(d, carry):
        @pl.when(d != k)
        def _():
            for i in range(2):
                c_copy(0, d, i, {"core": 1 - c}).wait_send()

        return carry

    lax.fori_loop(0, 8, drain_c, 0)


def on_device(gate_pre, up_pre, out_grad, down_weight):
    dma = pltpu.SemaphoreType.DMA
    any_spec = pl.BlockSpec(memory_space=pl.ANY)
    vmem = pl.BlockSpec(memory_space=pltpu.VMEM)
    act_shape = (32, 1664)
    return pl.pallas_call(
        kernel,
        out_shape=(
            jax.ShapeDtypeStruct((416, 1024), BF16),
            jax.ShapeDtypeStruct(act_shape, BF16),
            jax.ShapeDtypeStruct(act_shape, BF16),
        ),
        in_specs=[any_spec] * 4,
        out_specs=(vmem,) * 3,
        scratch_shapes=[
            pltpu.VMEM((4, 4, 4, 32, 1024), BF16),
            pltpu.VMEM((1664, 1024), BF16),
            pltpu.VMEM(act_shape, BF16),
            pltpu.VMEM(act_shape, BF16),
            pltpu.VMEM(act_shape, F32),
            pltpu.VMEM(act_shape, F32),
            pltpu.VMEM((4, 32, 512), BF16),
            pltpu.VMEM((4, 32, 512), BF16),
            pltpu.VMEM((16, 416, 128), BF16),
            pltpu.VMEM((8, 2, 32, 1664), F32),
            pltpu.VMEM((8, 2, 32, 1664), BF16),
            pltpu.VMEM((8, 32, 1664), BF16),
            pltpu.VMEM((2, 8, 32, 1664), BF16),
            pltpu.VMEM((8, 32, 1664), BF16),
            pltpu.VMEM(act_shape, F32),
            pltpu.VMEM((416, 1024), F32),
            dma((4,)),
            dma((2, 3)), dma((2, 3)),
            dma((4, 4)), dma((4, 4)),
            dma((4, 4)), dma((4, 4)),
            dma((3,)), dma((3,)),
            dma((16,)), dma((16,)),
            dma((16,)), dma((16,)),
            dma((8,)), dma((8,)),
            dma((4,)), dma((4,)),
            dma((8, 2)), dma((2, 8, 2)),
        ],
        compiler_params=pltpu.CompilerParams(
            collective_id=0, has_side_effects=True, vmem_limit_bytes=48 * 1024 * 1024
        ),
    )(gate_pre, up_pre, out_grad, down_weight)


def solution(mesh):
    torus = Mesh(mesh.devices.reshape(4, 4, 8, 2, 4), ("zh", "y", "zl", "core", "x"))
    in_specs = (
        P(("zl", "core", "x"), ROW),
        P(("zl", "core", "x"), ROW),
        P(("zh", "y", "x"), COL),
        P(ROW, COL),
    )
    out_specs = (P(("zh", "y", "x"), COL), P(("zl", "core", "x"), ROW), P(("zl", "core", "x"), ROW))
    return jax.shard_map(
        on_device, mesh=torus, in_specs=in_specs, out_specs=out_specs, check_vma=False
    )
```

```python
import functools

import jax
import jax.numpy as jnp
from jax import lax
from jax.experimental import pallas as pl
from jax.experimental.pallas import tpu as pltpu
from jax.sharding import Mesh
from jax.sharding import PartitionSpec as P

MESH = pl.DeviceIdType.MESH
COL = ("zl", "core")
ROW = ("zh", "y")
F32 = jnp.float32
BF16 = jnp.bfloat16
NT = (((1,), (1,)), ((), ()))
NB = 2


def kernel(
    gate_ref, up_ref, og_ref, w_ref,
    dw_ref, gg_ref, ug_ref,
    G, W, gv, uv, act, fac, HS, HX, HT, PF, PB, PR, RB, SB, HG, ACC,
    lsem, zs, zr, ys, yr, xs, xr, hs, hr, brs, brr, bls, blr, bps, bpr, ps, pr, cs, cr,
):
    zo, y, k, c, x = (lax.axis_index(a) for a in ("zh", "y", "zl", "core", "x"))
    zp, zm = lax.rem(zo + 1, 4), lax.rem(zo + 3, 4)
    yp, ym = lax.rem(y + 1, 4), lax.rem(y + 3, 4)
    xp, xm = lax.rem(x + 1, 4), lax.rem(x + 3, 4)
    sends = []

    def copy(src, dst, ss, rs, dev):
        return pltpu.make_async_remote_copy(
            src_ref=src, dst_ref=dst, send_sem=ss, recv_sem=rs, device_id=dev, device_id_type=MESH
        )

    def send(*args):
        cp = copy(*args)
        cp.start()
        sends.append(cp)

    barrier = pltpu.get_barrier_semaphore()
    peers = [{"zh": zp}, {"zh": zm}, {"y": yp}, {"y": ym}, {"x": xp}, {"x": xm},
             {"x": lax.rem(x + 2, 4)}, {"core": 1 - c}, {"zl": lax.rem(k + 1, 8)}, {"zl": lax.rem(k + 7, 8)}]
    for dev in peers:
        pl.semaphore_signal(barrier, inc=1, device_id=dev, device_id_type=MESH)
    loads = [
        pltpu.make_async_copy(og_ref, G.at[zo, y, x], lsem.at[0]),
        pltpu.make_async_copy(gate_ref, gv, lsem.at[1]),
        pltpu.make_async_copy(up_ref, uv, lsem.at[2]),
        pltpu.make_async_copy(w_ref, W, lsem.at[3]),
    ]
    for cp in loads:
        cp.start()
    loads[0].wait()
    pl.semaphore_wait(barrier, len(peers))

    def half(i):
        return pl.ds(16 * i, 16)

    def z_first():
        own = G.at[zo, y, x]
        for i, (hp, hm) in enumerate(((0, 1), (1, 0))):
            send(own.at[half(hp)], own.at[half(hp)], zs.at[0, i], zr.at[0, i], {"zh": zp})
            send(own.at[half(hm)], own.at[half(hm)], zs.at[1, i], zr.at[1, i], {"zh": zm})

    def z_wait(d, i):
        zh = (zm, zp)[d] if i < 2 else lax.rem(zo + 2, 4)
        hh = d if i != 1 else 1 - d
        dst = G.at[zh, y, x].at[half(hh)]
        copy(dst, dst, zs.at[d, i], zr.at[d, i], {"zh": zp}).wait_recv()

    def z_relay():
        z_wait(0, 0)
        r = G.at[zm, y, x].at[half(0)]
        send(r, r, zs.at[0, 2], zr.at[0, 2], {"zh": zp})
        z_wait(1, 0)
        r = G.at[zp, y, x].at[half(1)]
        send(r, r, zs.at[1, 2], zr.at[1, 2], {"zh": zm})
    def z_second():
        z_wait(0, 1)
        z_wait(1, 1)

    def y_first(q):
        b = G.at[lax.rem(zo + q, 4), y, x]
        send(b, b, ys.at[q, 0], yr.at[q, 0], {"y": yp})
        send(b, b, ys.at[q, 1], yr.at[q, 1], {"y": ym})

    def y_relay(q):
        zh = lax.rem(zo + q, 4)
        b = G.at[zh, ym, x]
        copy(b, b, ys.at[q, 0], yr.at[q, 0], {"y": yp}).wait_recv()
        b = b.at[half(0)]
        send(b, b, ys.at[q, 2], yr.at[q, 2], {"y": yp})
        b = G.at[zh, yp, x]
        copy(b, b, ys.at[q, 1], yr.at[q, 1], {"y": yp}).wait_recv()
        b = b.at[half(1)]
        send(b, b, ys.at[q, 3], yr.at[q, 3], {"y": ym})

    def y_last(q):
        b = G.at[lax.rem(zo + q, 4), lax.rem(y + 2, 4), x]
        for i in range(2):
            d = b.at[half(i)]
            copy(d, d, ys.at[q, 2 + i], yr.at[q, 2 + i], {"y": yp}).wait_recv()

    def x_first(q):
        b = G.at[lax.rem(zo + q, 4), :, x]
        send(b, b, xs.at[q, 0], xr.at[q, 0], {"x": xp})
        send(b, b, xs.at[q, 1], xr.at[q, 1], {"x": xm})

    def x_relay(q):
        zh = lax.rem(zo + q, 4)
        b = G.at[zh, :, xm]
        copy(b, b, xs.at[q, 0], xr.at[q, 0], {"x": xp}).wait_recv()
        b = G.at[zh, pl.ds(0, 2), xm]
        send(b, b, xs.at[q, 2], xr.at[q, 2], {"x": xp})
        b = G.at[zh, :, xp]
        copy(b, b, xs.at[q, 1], xr.at[q, 1], {"x": xp}).wait_recv()
        b = G.at[zh, pl.ds(2, 2), xp]
        send(b, b, xs.at[q, 3], xr.at[q, 3], {"x": xm})

    def x_last(q):
        zh = lax.rem(zo + q, 4)
        for i in range(2):
            d = G.at[zh, pl.ds(2 * i, 2), lax.rem(x + 2, 4)]
            copy(d, d, xs.at[q, 2 + i], xr.at[q, 2 + i], {"x": xp}).wait_recv()

    def hidden():
        loads[1].wait()
        loads[2].wait()
        g = gv[...].astype(F32)
        u = uv[...].astype(F32)
        sig = jax.nn.sigmoid(g)
        a = g * sig
        act[...] = a
        fac[...] = u * sig * (1.0 + g * (1.0 - sig))
        h = a * u
        for s in range(4):
            rolled = h if s == 0 else pltpu.roll(h, 1664 - 416 * s, 1)
            HS[s] = rolled[:, :512].astype(BF16)

    def h_first():
        for o in range(1, 4):
            to = lax.rem(x + o, 4)
            send(HS.at[to], HX.at[x], hs.at[o - 1], hr.at[o - 1], {"x": to})
        HX[x] = HS[x]

    def h_last():
        for o in range(1, 4):
            d = HX.at[lax.rem(x + 4 - o, 4)]
            copy(d, d, hs.at[o - 1], hr.at[o - 1], {"x": xp}).wait_recv()
        t = HX[...].astype(F32).reshape(128, 512).T
        HT[2 * k + c] = t[:416].astype(BF16)

    def ht(o, i):
        return HT.at[2 * o + c, pl.ds(416 // NB * i, 416 // NB)]

    def right(o, i, idx):
        b = ht(o, i)
        return copy(b, b, brs.at[idx], brr.at[idx], {"zl": k + 1})

    def left(o, i, idx):
        b = ht(o, i)
        return copy(b, b, bls.at[idx], blr.at[idx], {"zl": k - 1})

    def across(o):
        return copy(HT.at[2 * o + c], HT.at[2 * o + c], bps.at[o], bpr.at[o], {"core": 1 - c})

    def b_first():
        for i in range(NB):
            @pl.when(k < 7)
            def _():
                right(k, i, i).start()

            @pl.when(k > 0)
            def _():
                left(k, i, i).start()
        across(k).start()

    def b_steps(lo, hi):
        def step(s, carry):
            for i in range(NB):
                @pl.when(k - 1 - s >= 0)
                def _():
                    o = k - 1 - s
                    right(o, i, NB * s + i).wait_recv()

                    @pl.when(k < 7)
                    def _():
                        right(o, i, NB * s + NB + i).start()

                @pl.when(k + 1 + s <= 7)
                def _():
                    o = k + 1 + s
                    left(o, i, NB * s + i).wait_recv()

                    @pl.when(k > 0)
                    def _():
                        left(o, i, NB * s + NB + i).start()

            @pl.when(k - 1 - s >= 0)
            def _():
                across(k - 1 - s).start()

            @pl.when(k + 1 + s <= 7)
            def _():
                across(k + 1 + s).start()

            return carry

        lax.fori_loop(lo, hi, step, 0)

    def b_last():
        def step(o, carry):
            d = HT.at[2 * o + 1 - c]
            copy(d, d, bps.at[o], bpr.at[o], {"core": 1 - c}).wait_recv()
            return carry

        lax.fori_loop(0, 8, step, 0)

    def terms(q):
        zh = lax.rem(zo + q, 4)
        rows = G[zh, :, x].reshape(128, 1024)

        def part(n0, nn):
            res = lax.dot_general(rows, W[pl.ds(n0, nn), :], NT, preferred_element_type=F32)
            res = res.reshape(2, 2, 32, nn)
            PF[pl.ds(2 * zh, 2), :, :, pl.ds(n0, nn)] = res
            PB[pl.ds(2 * zh, 2), :, :, pl.ds(n0, nn)] = res.astype(BF16)

        def step(i, carry):
            part(pl.multiple_of(i * 256, 256), 256)
            return carry

        lax.fori_loop(0, 6, step, 0)
        part(1536, 128)
        send(PB.at[pl.ds(2 * zh, 2), 1 - c], PR.at[pl.ds(2 * zh, 2)], ps.at[q], pr.at[q], {"core": 1 - c})

    def terms_last(q):
        zh = lax.rem(zo + q, 4)
        d = PR.at[pl.ds(2 * zh, 2)]
        copy(d, d, ps.at[q], pr.at[q], {"core": 1 - c}).wait_recv()

    def quarter(i):
        return pl.ds(8 * i, 8)

    def c_copy(way, d, i, dev):
        return copy(SB.at[d, quarter(i)], RB.at[way, d, quarter(i)], cs.at[d, i], cr.at[way, d, i], dev)

    def c_send(way, pos, d, to):
        for i in range(4):
            mine = PF[d, c, quarter(i)] + PR[d, quarter(i)].astype(F32)

            @pl.when(pos == 0)
            def _():
                SB[d, quarter(i)] = mine.astype(BF16)

            @pl.when(pos > 0)
            def _():
                c_copy(way, d, i, {"zl": to}).wait_recv()
                SB[d, quarter(i)] = (mine + RB[way, d, quarter(i)].astype(F32)).astype(BF16)

            c_copy(way, d, i, {"zl": to}).start()

    def c_steps(lo, hi):
        def step(t, carry):
            @pl.when((t >= k) & (k < 7))
            def _():
                c_send(0, k, 7 + k - t, k + 1)

            @pl.when((t >= 7 - k) & (k > 0))
            def _():
                c_send(1, 7 - k, t - 7 + k, k - 1)

            return carry

        lax.fori_loop(lo, hi, step, 0)

    def c_last():
        HG[...] = PF[k, c] + PR[k].astype(F32)

        @pl.when(k > 0)
        def _():
            for i in range(4):
                c_copy(0, k, i, {"zl": k - 1}).wait_recv()
            HG[...] += RB[0, k].astype(F32)

        @pl.when(k < 7)
        def _():
            for i in range(4):
                c_copy(1, k, i, {"zl": k + 1}).wait_recv()
            HG[...] += RB[1, k].astype(F32)

        hg = HG[...]
        ug_ref[...] = (hg * act[...]).astype(BF16)
        gg_ref[...] = (hg * fac[...]).astype(BF16)

    def dw(q, first=False, last=False):
        zh = lax.rem(zo + q, 4)
        lhs = jnp.concatenate([HT[4 * zh + i] for i in range(4)], axis=1)

        def step(n, carry):
            cols = pl.ds(pl.multiple_of(n * 256, 256), 256)
            rhs = G[zh, :, :, :, cols].reshape(512, 256)
            res = jnp.dot(lhs, rhs, preferred_element_type=F32)
            if last:
                dw_ref[:, cols] = (ACC[:, cols] + res).astype(BF16)
            else:
                ACC[:, cols] = res if first else ACC[:, cols] + res
            return carry

        lax.fori_loop(0, 4, step, 0)

    z_first()
    y_first(0)
    hidden()
    h_first()
    h_last()
    b_first()
    y_relay(0)
    y_last(0)
    x_first(0)
    loads[3].wait()
    terms(0)
    b_steps(0,2)
    z_relay()
    z_second()
    y_first(1)
    y_first(3)
    y_relay(1)
    y_relay(3)
    y_last(1)
    y_last(3)
    x_first(1)
    x_first(3)
    x_relay(0)
    z_wait(0,2)
    z_wait(1,2)
    y_first(2)
    terms(1)
    terms(3)
    y_relay(2)
    y_last(2)
    x_first(2)
    terms(2)
    terms_last(0)
    terms_last(1)
    terms_last(3)
    terms_last(2)
    c_steps(0,1)
    b_steps(2,3)
    c_steps(1,2)
    x_relay(1)
    b_steps(3,4)
    c_steps(2,3)
    x_relay(3)
    b_steps(4,5)
    c_steps(3,4)
    b_steps(5,6)
    c_steps(4,5)
    x_relay(2)
    b_steps(6,7)
    c_steps(5,6)
    c_steps(6,7)
    c_last()
    b_last()
    x_last(0)
    dw(0,first=True)
    x_last(1)
    dw(1)
    x_last(3)
    dw(3)
    x_last(2)
    dw(2,last=True)

    for cp in sends:
        cp.wait_send()

    def drain_b(s, carry):
        for i in range(NB):
            @pl.when((k - s >= 0) & (k < 7))
            def _():
                right(k - s, i, NB * s + i).wait_send()

            @pl.when((k + s <= 7) & (k > 0))
            def _():
                left(k + s, i, NB * s + i).wait_send()

        across(s).wait_send()
        return carry

    lax.fori_loop(0, 8, drain_b, 0)

    def drain_c(d, carry):
        @pl.when(d != k)
        def _():
            for i in range(4):
                c_copy(0, d, i, {"core": 1 - c}).wait_send()

        return carry

    lax.fori_loop(0, 8, drain_c, 0)


def on_device(gate_pre, up_pre, out_grad, down_weight):
    dma = pltpu.SemaphoreType.DMA
    hbm = pl.BlockSpec(memory_space=pltpu.MemorySpace.HBM)
    vmem = pl.BlockSpec(memory_space=pltpu.VMEM)
    act_shape = (32, 1664)
    return pl.pallas_call(
        kernel,
        out_shape=(
            jax.ShapeDtypeStruct((416, 1024), BF16),
            jax.ShapeDtypeStruct(act_shape, BF16),
            jax.ShapeDtypeStruct(act_shape, BF16),
        ),
        in_specs=[hbm] * 4,
        out_specs=(vmem,) * 3,
        scratch_shapes=[
            pltpu.VMEM((4, 4, 4, 32, 1024), BF16),
            pltpu.VMEM((1664, 1024), BF16),
            pltpu.VMEM(act_shape, BF16),
            pltpu.VMEM(act_shape, BF16),
            pltpu.VMEM(act_shape, F32),
            pltpu.VMEM(act_shape, F32),
            pltpu.VMEM((4, 32, 512), BF16),
            pltpu.VMEM((4, 32, 512), BF16),
            pltpu.VMEM((16, 416, 128), BF16),
            pltpu.VMEM((8, 2, 32, 1664), F32),
            pltpu.VMEM((8, 2, 32, 1664), BF16),
            pltpu.VMEM((8, 32, 1664), BF16),
            pltpu.VMEM((2, 8, 32, 1664), BF16),
            pltpu.VMEM((8, 32, 1664), BF16),
            pltpu.VMEM(act_shape, F32),
            pltpu.VMEM((416, 1024), F32),
            dma((4,)),
            dma((2, 3)), dma((2, 3)),
            dma((4, 4)), dma((4, 4)),
            dma((4, 4)), dma((4, 4)),
            dma((3,)), dma((3,)),
            dma((8 * NB,)), dma((8 * NB,)),
            dma((8 * NB,)), dma((8 * NB,)),
            dma((8,)), dma((8,)),
            dma((4,)), dma((4,)),
            dma((8, 4)), dma((2, 8, 4)),
        ],
        compiler_params=pltpu.CompilerParams(
            collective_id=0, has_side_effects=True, vmem_limit_bytes=67043328
        ),
    )(gate_pre, up_pre, out_grad, down_weight)


def solution(mesh):
    torus = Mesh(mesh.devices.reshape(4, 4, 8, 2, 4), ("zh", "y", "zl", "core", "x"))
    in_specs = (
        P(("zl", "core", "x"), ROW),
        P(("zl", "core", "x"), ROW),
        P(("zh", "y", "x"), COL),
        P(ROW, COL),
    )
    out_specs = (P(("zh", "y", "x"), COL), P(("zl", "core", "x"), ROW), P(("zl", "core", "x"), ROW))
    return jax.shard_map(
        on_device, mesh=torus, in_specs=in_specs, out_specs=out_specs, check_vma=False
    )
```

```python
import functools

import jax
import jax.numpy as jnp
from jax import lax
from jax.experimental import pallas as pl
from jax.experimental.pallas import tpu as pltpu
from jax.sharding import Mesh
from jax.sharding import PartitionSpec as P

MESH = pl.DeviceIdType.MESH
COL = ("zl", "core")
ROW = ("zh", "y")
F32 = jnp.float32
BF16 = jnp.bfloat16
NT = (((1,), (1,)), ((), ()))
NB = 2


def kernel(
    gate_ref, up_ref, og_ref, w_ref,
    dw_ref, hg_ref,
    G, W, gv, uv, HS, HX, HT, PF, PB, PR, RB, SB, ACC,
    lsem, zs, zr, ys, yr, xs, xr, hs, hr, brs, brr, bls, blr, bps, bpr, ps, pr, cs, cr,
):
    zo, y, k, c, x = (lax.axis_index(a) for a in ("zh", "y", "zl", "core", "x"))
    zp, zm = lax.rem(zo + 1, 4), lax.rem(zo + 3, 4)
    yp, ym = lax.rem(y + 1, 4), lax.rem(y + 3, 4)
    xp, xm = lax.rem(x + 1, 4), lax.rem(x + 3, 4)
    sends = []

    def copy(src, dst, ss, rs, dev):
        return pltpu.make_async_remote_copy(
            src_ref=src, dst_ref=dst, send_sem=ss, recv_sem=rs, device_id=dev, device_id_type=MESH
        )

    def send(*args):
        cp = copy(*args)
        cp.start()
        sends.append(cp)

    barrier = pltpu.get_barrier_semaphore()
    peers = [{"zh": zp}, {"zh": zm}, {"y": yp}, {"y": ym}, {"x": xp}, {"x": xm},
             {"x": lax.rem(x + 2, 4)}, {"core": 1 - c}, {"zl": lax.rem(k + 1, 8)}, {"zl": lax.rem(k + 7, 8)}]
    for dev in peers:
        pl.semaphore_signal(barrier, inc=1, device_id=dev, device_id_type=MESH)
    loads = [
        pltpu.make_async_copy(og_ref, G.at[zo, y, x], lsem.at[0]),
        pltpu.make_async_copy(gate_ref, gv, lsem.at[1]),
        pltpu.make_async_copy(up_ref, uv, lsem.at[2]),
        pltpu.make_async_copy(w_ref, W, lsem.at[3]),
    ]
    for cp in loads:
        cp.start()
    loads[0].wait()
    pl.semaphore_wait(barrier, len(peers))

    def half(i):
        return pl.ds(16 * i, 16)

    def z_first():
        own = G.at[zo, y, x]
        for i, (hp, hm) in enumerate(((0, 1), (1, 0))):
            send(own.at[half(hp)], own.at[half(hp)], zs.at[0, i], zr.at[0, i], {"zh": zp})
            send(own.at[half(hm)], own.at[half(hm)], zs.at[1, i], zr.at[1, i], {"zh": zm})

    def z_wait(d, i):
        zh = (zm, zp)[d] if i < 2 else lax.rem(zo + 2, 4)
        hh = d if i != 1 else 1 - d
        dst = G.at[zh, y, x].at[half(hh)]
        copy(dst, dst, zs.at[d, i], zr.at[d, i], {"zh": zp}).wait_recv()

    def z_relay():
        z_wait(0, 0)
        r = G.at[zm, y, x].at[half(0)]
        send(r, r, zs.at[0, 2], zr.at[0, 2], {"zh": zp})
        z_wait(1, 0)
        r = G.at[zp, y, x].at[half(1)]
        send(r, r, zs.at[1, 2], zr.at[1, 2], {"zh": zm})
    def z_second():
        z_wait(0, 1)
        z_wait(1, 1)

    def y_first(q):
        b = G.at[lax.rem(zo + q, 4), y, x]
        send(b, b, ys.at[q, 0], yr.at[q, 0], {"y": yp})
        send(b, b, ys.at[q, 1], yr.at[q, 1], {"y": ym})

    def y_relay(q):
        zh = lax.rem(zo + q, 4)
        b = G.at[zh, ym, x]
        copy(b, b, ys.at[q, 0], yr.at[q, 0], {"y": yp}).wait_recv()
        b = b.at[half(0)]
        send(b, b, ys.at[q, 2], yr.at[q, 2], {"y": yp})
        b = G.at[zh, yp, x]
        copy(b, b, ys.at[q, 1], yr.at[q, 1], {"y": yp}).wait_recv()
        b = b.at[half(1)]
        send(b, b, ys.at[q, 3], yr.at[q, 3], {"y": ym})

    def y_last(q):
        b = G.at[lax.rem(zo + q, 4), lax.rem(y + 2, 4), x]
        for i in range(2):
            d = b.at[half(i)]
            copy(d, d, ys.at[q, 2 + i], yr.at[q, 2 + i], {"y": yp}).wait_recv()

    def x_first(q):
        b = G.at[lax.rem(zo + q, 4), :, x]
        send(b, b, xs.at[q, 0], xr.at[q, 0], {"x": xp})
        send(b, b, xs.at[q, 1], xr.at[q, 1], {"x": xm})

    def x_relay(q):
        zh = lax.rem(zo + q, 4)
        b = G.at[zh, :, xm]
        copy(b, b, xs.at[q, 0], xr.at[q, 0], {"x": xp}).wait_recv()
        b = G.at[zh, pl.ds(0, 2), xm]
        send(b, b, xs.at[q, 2], xr.at[q, 2], {"x": xp})
        b = G.at[zh, :, xp]
        copy(b, b, xs.at[q, 1], xr.at[q, 1], {"x": xp}).wait_recv()
        b = G.at[zh, pl.ds(2, 2), xp]
        send(b, b, xs.at[q, 3], xr.at[q, 3], {"x": xm})

    def x_last(q):
        zh = lax.rem(zo + q, 4)
        for i in range(2):
            d = G.at[zh, pl.ds(2 * i, 2), lax.rem(x + 2, 4)]
            copy(d, d, xs.at[q, 2 + i], xr.at[q, 2 + i], {"x": xp}).wait_recv()

    def hidden():
        loads[1].wait()
        loads[2].wait()
        g = gv[...].astype(F32)
        u = uv[...].astype(F32)
        sig = jax.nn.sigmoid(g)
        h = g * sig * u
        for s in range(4):
            rolled = h if s == 0 else pltpu.roll(h, 1664 - 416 * s, 1)
            HS[s] = rolled[:, :512].astype(BF16)

    def h_first():
        for o in range(1, 4):
            to = lax.rem(x + o, 4)
            send(HS.at[to], HX.at[x], hs.at[o - 1], hr.at[o - 1], {"x": to})
        HX[x] = HS[x]

    def h_last():
        for o in range(1, 4):
            d = HX.at[lax.rem(x + 4 - o, 4)]
            copy(d, d, hs.at[o - 1], hr.at[o - 1], {"x": xp}).wait_recv()
        t = HX[...].astype(F32).reshape(128, 512).T
        HT[2 * k + c] = t[:416].astype(BF16)

    def ht(o, i):
        return HT.at[2 * o + c, pl.ds(416 // NB * i, 416 // NB)]

    def right(o, i, idx):
        b = ht(o, i)
        return copy(b, b, brs.at[idx], brr.at[idx], {"zl": k + 1})

    def left(o, i, idx):
        b = ht(o, i)
        return copy(b, b, bls.at[idx], blr.at[idx], {"zl": k - 1})

    def across(o):
        return copy(HT.at[2 * o + c], HT.at[2 * o + c], bps.at[o], bpr.at[o], {"core": 1 - c})

    def b_first():
        for i in range(NB):
            @pl.when(k < 7)
            def _():
                right(k, i, i).start()

            @pl.when(k > 0)
            def _():
                left(k, i, i).start()
        across(k).start()

    def b_steps(lo, hi):
        def step(s, carry):
            for i in range(NB):
                @pl.when(k - 1 - s >= 0)
                def _():
                    o = k - 1 - s
                    right(o, i, NB * s + i).wait_recv()

                    @pl.when(k < 7)
                    def _():
                        right(o, i, NB * s + NB + i).start()

                @pl.when(k + 1 + s <= 7)
                def _():
                    o = k + 1 + s
                    left(o, i, NB * s + i).wait_recv()

                    @pl.when(k > 0)
                    def _():
                        left(o, i, NB * s + NB + i).start()

            @pl.when(k - 1 - s >= 0)
            def _():
                across(k - 1 - s).start()

            @pl.when(k + 1 + s <= 7)
            def _():
                across(k + 1 + s).start()

            return carry

        lax.fori_loop(lo, hi, step, 0)

    def b_last():
        def step(o, carry):
            d = HT.at[2 * o + 1 - c]
            copy(d, d, bps.at[o], bpr.at[o], {"core": 1 - c}).wait_recv()
            return carry

        lax.fori_loop(0, 8, step, 0)

    def terms(*groups):
        zhs = [lax.rem(zo + q, 4) for q in groups]
        rows = jnp.concatenate([G[zh, :, x].reshape(128, 1024) for zh in zhs], axis=0)

        def part(n0, nn):
            res = lax.dot_general(rows, W[pl.ds(n0, nn), :], NT, preferred_element_type=F32)
            for n, zh in enumerate(zhs):
                one = res[128 * n : 128 * n + 128].reshape(2, 2, 32, nn)
                PF[pl.ds(2 * zh, 2), :, :, pl.ds(n0, nn)] = one
                PB[pl.ds(2 * zh, 2), :, :, pl.ds(n0, nn)] = one.astype(BF16)

        def step(i, carry):
            part(pl.multiple_of(i * 256, 256), 256)
            return carry

        lax.fori_loop(0, 6, step, 0)
        part(1536, 128)
        for q, zh in zip(groups, zhs):
            pair = PB.at[pl.ds(2 * zh, 2), 1 - c]
            send(pair, PR.at[pl.ds(2 * zh, 2)], ps.at[q], pr.at[q], {"core": 1 - c})

    def terms_last(q):
        zh = lax.rem(zo + q, 4)
        d = PR.at[pl.ds(2 * zh, 2)]
        copy(d, d, ps.at[q], pr.at[q], {"core": 1 - c}).wait_recv()

    def quarter(i):
        return pl.ds(8 * i, 8)

    def c_copy(way, d, i, dev):
        return copy(SB.at[d, quarter(i)], RB.at[way, d, quarter(i)], cs.at[d, i], cr.at[way, d, i], dev)

    def c_send(way, pos, d, to):
        for i in range(4):
            mine = PF[d, c, quarter(i)] + PR[d, quarter(i)].astype(F32)

            @pl.when(pos == 0)
            def _():
                SB[d, quarter(i)] = mine.astype(BF16)

            @pl.when(pos > 0)
            def _():
                c_copy(way, d, i, {"zl": to}).wait_recv()
                SB[d, quarter(i)] = (mine + RB[way, d, quarter(i)].astype(F32)).astype(BF16)

            c_copy(way, d, i, {"zl": to}).start()

    def c_steps(lo, hi):
        def step(t, carry):
            @pl.when((t >= k) & (k < 7))
            def _():
                c_send(0, k, 7 + k - t, k + 1)

            @pl.when((t >= 7 - k) & (k > 0))
            def _():
                c_send(1, 7 - k, t - 7 + k, k - 1)

            return carry

        lax.fori_loop(lo, hi, step, 0)

    def c_last():
        hg_ref[...] = PF[k, c] + PR[k].astype(F32)

        @pl.when(k > 0)
        def _():
            for i in range(4):
                c_copy(0, k, i, {"zl": k - 1}).wait_recv()
            hg_ref[...] += RB[0, k].astype(F32)

        @pl.when(k < 7)
        def _():
            for i in range(4):
                c_copy(1, k, i, {"zl": k + 1}).wait_recv()
            hg_ref[...] += RB[1, k].astype(F32)


    def dw(q, first=False, last=False):
        zh = lax.rem(zo + q, 4)
        lhs = jnp.concatenate([HT[4 * zh + i] for i in range(4)], axis=1)

        def step(n, carry):
            cols = pl.ds(pl.multiple_of(n * 256, 256), 256)
            rhs = G[zh, :, :, :, cols].reshape(512, 256)
            res = jnp.dot(lhs, rhs, preferred_element_type=F32)
            if last:
                dw_ref[:, cols] = (ACC[:, cols] + res).astype(BF16)
            else:
                ACC[:, cols] = res if first else ACC[:, cols] + res
            return carry

        lax.fori_loop(0, 4, step, 0)

    z_first()
    y_first(0)
    hidden()
    h_first()
    h_last()
    b_first()
    y_relay(0)
    y_last(0)
    x_first(0)
    b_steps(0,1)
    z_relay()
    loads[3].wait()
    terms(0)
    b_steps(1,2)
    z_second()
    y_first(1)
    y_first(3)
    y_relay(1)
    y_relay(3)
    z_wait(0,2)
    z_wait(1,2)
    y_first(2)
    y_last(1)
    y_last(3)
    x_first(1)
    x_first(3)
    terms(1,3)
    y_relay(2)
    y_last(2)
    x_first(2)
    terms(2)
    x_relay(0)
    terms_last(0)
    terms_last(1)
    terms_last(3)
    terms_last(2)
    c_steps(0,1)
    b_steps(2,3)
    c_steps(1,2)
    x_relay(1)
    b_steps(3,4)
    c_steps(2,3)
    x_relay(3)
    b_steps(4,5)
    c_steps(3,4)
    b_steps(5,6)
    c_steps(4,5)
    x_relay(2)
    b_steps(6,7)
    c_steps(5,6)
    b_last()
    x_last(0)
    dw(0,first=True)
    c_steps(6,7)
    x_last(1)
    dw(1)
    c_last()
    x_last(3)
    dw(3)
    x_last(2)
    dw(2,last=True)

    for cp in sends:
        cp.wait_send()

    def drain_b(s, carry):
        for i in range(NB):
            @pl.when((k - s >= 0) & (k < 7))
            def _():
                right(k - s, i, NB * s + i).wait_send()

            @pl.when((k + s <= 7) & (k > 0))
            def _():
                left(k + s, i, NB * s + i).wait_send()

        across(s).wait_send()
        return carry

    lax.fori_loop(0, 8, drain_b, 0)

    def drain_c(d, carry):
        @pl.when(d != k)
        def _():
            for i in range(4):
                c_copy(0, d, i, {"core": 1 - c}).wait_send()

        return carry

    lax.fori_loop(0, 8, drain_c, 0)


def on_device(gate_pre, up_pre, out_grad, down_weight):
    dma = pltpu.SemaphoreType.DMA
    hbm = pl.BlockSpec(memory_space=pltpu.MemorySpace.HBM)
    vmem = pl.BlockSpec(memory_space=pltpu.VMEM)
    act_shape = (32, 1664)
    weight_grad, hidden_grad = pl.pallas_call(
        kernel,
        out_shape=(
            jax.ShapeDtypeStruct((416, 1024), BF16),
            jax.ShapeDtypeStruct(act_shape, F32),
        ),
        in_specs=[hbm] * 4,
        out_specs=(vmem,) * 2,
        scratch_shapes=[
            pltpu.VMEM((4, 4, 4, 32, 1024), BF16),
            pltpu.VMEM((1664, 1024), BF16),
            pltpu.VMEM(act_shape, BF16),
            pltpu.VMEM(act_shape, BF16),
            pltpu.VMEM((4, 32, 512), BF16),
            pltpu.VMEM((4, 32, 512), BF16),
            pltpu.VMEM((16, 416, 128), BF16),
            pltpu.VMEM((8, 2, 32, 1664), F32),
            pltpu.VMEM((8, 2, 32, 1664), BF16),
            pltpu.VMEM((8, 32, 1664), BF16),
            pltpu.VMEM((2, 8, 32, 1664), BF16),
            pltpu.VMEM((8, 32, 1664), BF16),
            pltpu.VMEM((416, 1024), F32),
            dma((4,)),
            dma((2, 3)), dma((2, 3)),
            dma((4, 4)), dma((4, 4)),
            dma((4, 4)), dma((4, 4)),
            dma((3,)), dma((3,)),
            dma((8 * NB,)), dma((8 * NB,)),
            dma((8 * NB,)), dma((8 * NB,)),
            dma((8,)), dma((8,)),
            dma((4,)), dma((4,)),
            dma((8, 4)), dma((2, 8, 4)),
        ],
        compiler_params=pltpu.CompilerParams(
            collective_id=0, has_side_effects=True, vmem_limit_bytes=67043328
        ),
    )(gate_pre, up_pre, out_grad, down_weight)
    gate_vals = gate_pre.astype(F32)
    sigma = jax.nn.sigmoid(gate_vals)
    up_grad = (hidden_grad * (gate_vals * sigma)).astype(BF16)
    slope = up_pre.astype(F32) * sigma * (1.0 + gate_vals * (1.0 - sigma))
    gate_grad = (hidden_grad * slope).astype(BF16)
    return weight_grad, gate_grad, up_grad


def solution(mesh):
    torus = Mesh(mesh.devices.reshape(4, 4, 8, 2, 4), ("zh", "y", "zl", "core", "x"))
    in_specs = (
        P(("zl", "core", "x"), ROW),
        P(("zl", "core", "x"), ROW),
        P(("zh", "y", "x"), COL),
        P(ROW, COL),
    )
    out_specs = (P(("zh", "y", "x"), COL), P(("zl", "core", "x"), ROW), P(("zl", "core", "x"), ROW))
    return jax.shard_map(
        on_device, mesh=torus, in_specs=in_specs, out_specs=out_specs, check_vma=False
    )
```

```python
import functools

import jax
import jax.numpy as jnp
from jax import lax
from jax.experimental import pallas as pl
from jax.experimental.pallas import tpu as pltpu
from jax.sharding import Mesh
from jax.sharding import PartitionSpec as P

MESH = pl.DeviceIdType.MESH
COL = ("zl", "core")
ROW = ("zh", "y")
F32 = jnp.float32
BF16 = jnp.bfloat16
NT = (((1,), (1,)), ((), ()))
NB = 2


def kernel(
    gate_ref, up_ref, og_ref, w_ref,
    dw_ref, hg_ref,
    G, W, gv, uv, HS, HX, HT, PF, PB, PR, RB, SB, ACC,
    lsem, zs, zr, ys, yr, xs, xr, hs, hr, brs, brr, bls, blr, bps, bpr, ps, pr, cs, cr,
):
    zo, y, k, c, x = (lax.axis_index(a) for a in ("zh", "y", "zl", "core", "x"))
    zp, zm = lax.rem(zo + 1, 4), lax.rem(zo + 3, 4)
    yp, ym = lax.rem(y + 1, 4), lax.rem(y + 3, 4)
    xp, xm = lax.rem(x + 1, 4), lax.rem(x + 3, 4)
    sends = []

    def copy(src, dst, ss, rs, dev):
        return pltpu.make_async_remote_copy(
            src_ref=src, dst_ref=dst, send_sem=ss, recv_sem=rs, device_id=dev, device_id_type=MESH
        )

    def send(*args):
        cp = copy(*args)
        cp.start()
        sends.append(cp)

    barrier = pltpu.get_barrier_semaphore()
    peers = [{"zh": zp}, {"zh": zm}, {"y": yp}, {"y": ym}, {"x": xp}, {"x": xm},
             {"x": lax.rem(x + 2, 4)}, {"core": 1 - c}, {"zl": lax.rem(k + 1, 8)}, {"zl": lax.rem(k + 7, 8)}]
    for dev in peers:
        pl.semaphore_signal(barrier, inc=1, device_id=dev, device_id_type=MESH)
    loads = [
        pltpu.make_async_copy(og_ref, G.at[zo, y, x], lsem.at[0]),
        pltpu.make_async_copy(gate_ref, gv, lsem.at[1]),
        pltpu.make_async_copy(up_ref, uv, lsem.at[2]),
        pltpu.make_async_copy(w_ref, W, lsem.at[3]),
    ]
    for cp in loads:
        cp.start()
    loads[0].wait()
    pl.semaphore_wait(barrier, len(peers))

    def half(i):
        return pl.ds(16 * i, 16)

    def z_first():
        own = G.at[zo, y, x]
        for i, (hp, hm) in enumerate(((0, 1), (1, 0))):
            send(own.at[half(hp)], own.at[half(hp)], zs.at[0, i], zr.at[0, i], {"zh": zp})
            send(own.at[half(hm)], own.at[half(hm)], zs.at[1, i], zr.at[1, i], {"zh": zm})

    def z_wait(d, i):
        zh = (zm, zp)[d] if i < 2 else lax.rem(zo + 2, 4)
        hh = d if i != 1 else 1 - d
        dst = G.at[zh, y, x].at[half(hh)]
        copy(dst, dst, zs.at[d, i], zr.at[d, i], {"zh": zp}).wait_recv()

    def z_relay():
        z_wait(0, 0)
        r = G.at[zm, y, x].at[half(0)]
        send(r, r, zs.at[0, 2], zr.at[0, 2], {"zh": zp})
        z_wait(1, 0)
        r = G.at[zp, y, x].at[half(1)]
        send(r, r, zs.at[1, 2], zr.at[1, 2], {"zh": zm})
    def z_second():
        z_wait(0, 1)
        z_wait(1, 1)

    def y_first(q):
        b = G.at[lax.rem(zo + q, 4), y, x]
        send(b, b, ys.at[q, 0], yr.at[q, 0], {"y": yp})
        send(b, b, ys.at[q, 1], yr.at[q, 1], {"y": ym})

    def y_relay(q):
        zh = lax.rem(zo + q, 4)
        b = G.at[zh, ym, x]
        copy(b, b, ys.at[q, 0], yr.at[q, 0], {"y": yp}).wait_recv()
        b = b.at[half(0)]
        send(b, b, ys.at[q, 2], yr.at[q, 2], {"y": yp})
        b = G.at[zh, yp, x]
        copy(b, b, ys.at[q, 1], yr.at[q, 1], {"y": yp}).wait_recv()
        b = b.at[half(1)]
        send(b, b, ys.at[q, 3], yr.at[q, 3], {"y": ym})

    def y_last(q):
        b = G.at[lax.rem(zo + q, 4), lax.rem(y + 2, 4), x]
        for i in range(2):
            d = b.at[half(i)]
            copy(d, d, ys.at[q, 2 + i], yr.at[q, 2 + i], {"y": yp}).wait_recv()

    def x_first(q):
        b = G.at[lax.rem(zo + q, 4), :, x]
        send(b, b, xs.at[q, 0], xr.at[q, 0], {"x": xp})
        send(b, b, xs.at[q, 1], xr.at[q, 1], {"x": xm})

    def x_relay(q):
        zh = lax.rem(zo + q, 4)
        b = G.at[zh, :, xm]
        copy(b, b, xs.at[q, 0], xr.at[q, 0], {"x": xp}).wait_recv()
        b = G.at[zh, pl.ds(0, 2), xm]
        send(b, b, xs.at[q, 2], xr.at[q, 2], {"x": xp})
        b = G.at[zh, :, xp]
        copy(b, b, xs.at[q, 1], xr.at[q, 1], {"x": xp}).wait_recv()
        b = G.at[zh, pl.ds(2, 2), xp]
        send(b, b, xs.at[q, 3], xr.at[q, 3], {"x": xm})

    def x_last(q):
        zh = lax.rem(zo + q, 4)
        for i in range(2):
            d = G.at[zh, pl.ds(2 * i, 2), lax.rem(x + 2, 4)]
            copy(d, d, xs.at[q, 2 + i], xr.at[q, 2 + i], {"x": xp}).wait_recv()

    def hidden():
        loads[1].wait()
        loads[2].wait()
        g = gv[...].astype(F32)
        u = uv[...].astype(F32)
        sig = jax.nn.sigmoid(g)
        h = g * sig * u
        for s in range(4):
            rolled = h if s == 0 else pltpu.roll(h, 1664 - 416 * s, 1)
            HS[s] = rolled[:, :512].astype(BF16)

    def h_first():
        for o in range(1, 4):
            to = lax.rem(x + o, 4)
            send(HS.at[to], HX.at[x], hs.at[o - 1], hr.at[o - 1], {"x": to})
        HX[x] = HS[x]

    def h_last():
        for o in range(1, 4):
            d = HX.at[lax.rem(x + 4 - o, 4)]
            copy(d, d, hs.at[o - 1], hr.at[o - 1], {"x": xp}).wait_recv()
        t = HX[...].astype(F32).reshape(128, 512).T
        HT[2 * k + c] = t[:416].astype(BF16)

    def ht(o, i):
        return HT.at[2 * o + c, pl.ds(416 // NB * i, 416 // NB)]

    def right(o, i, idx):
        b = ht(o, i)
        return copy(b, b, brs.at[idx], brr.at[idx], {"zl": k + 1})

    def left(o, i, idx):
        b = ht(o, i)
        return copy(b, b, bls.at[idx], blr.at[idx], {"zl": k - 1})

    def across(o):
        return copy(HT.at[2 * o + c], HT.at[2 * o + c], bps.at[o], bpr.at[o], {"core": 1 - c})

    def b_first():
        for i in range(NB):
            @pl.when(k < 7)
            def _():
                right(k, i, i).start()

            @pl.when(k > 0)
            def _():
                left(k, i, i).start()
        across(k).start()

    def b_steps(lo, hi):
        def step(s, carry):
            for i in range(NB):
                @pl.when(k - 1 - s >= 0)
                def _():
                    o = k - 1 - s
                    right(o, i, NB * s + i).wait_recv()

                    @pl.when(k < 7)
                    def _():
                        right(o, i, NB * s + NB + i).start()

                @pl.when(k + 1 + s <= 7)
                def _():
                    o = k + 1 + s
                    left(o, i, NB * s + i).wait_recv()

                    @pl.when(k > 0)
                    def _():
                        left(o, i, NB * s + NB + i).start()

            @pl.when(k - 1 - s >= 0)
            def _():
                across(k - 1 - s).start()

            @pl.when(k + 1 + s <= 7)
            def _():
                across(k + 1 + s).start()

            return carry

        lax.fori_loop(lo, hi, step, 0)

    def b_last():
        def step(o, carry):
            d = HT.at[2 * o + 1 - c]
            copy(d, d, bps.at[o], bpr.at[o], {"core": 1 - c}).wait_recv()
            return carry

        lax.fori_loop(0, 8, step, 0)

    def terms(*groups):
        zhs = [lax.rem(zo + q, 4) for q in groups]
        rows = jnp.concatenate([G[zh, :, x].reshape(128, 1024) for zh in zhs], axis=0)

        def part(n0, nn):
            res = lax.dot_general(rows, W[pl.ds(n0, nn), :], NT, preferred_element_type=F32)
            for n, zh in enumerate(zhs):
                one = res[128 * n : 128 * n + 128].reshape(2, 2, 32, nn)
                PF[pl.ds(2 * zh, 2), :, :, pl.ds(n0, nn)] = one
                PB[pl.ds(2 * zh, 2), :, :, pl.ds(n0, nn)] = one.astype(BF16)

        def step(i, carry):
            part(pl.multiple_of(i * 256, 256), 256)
            return carry

        lax.fori_loop(0, 6, step, 0)
        part(1536, 128)
        for q, zh in zip(groups, zhs):
            pair = PB.at[pl.ds(2 * zh, 2), 1 - c]
            send(pair, PR.at[pl.ds(2 * zh, 2)], ps.at[q], pr.at[q], {"core": 1 - c})

    def terms_last(q):
        zh = lax.rem(zo + q, 4)
        d = PR.at[pl.ds(2 * zh, 2)]
        copy(d, d, ps.at[q], pr.at[q], {"core": 1 - c}).wait_recv()

    def quarter(i):
        return pl.ds(8 * i, 8)

    def c_copy(way, d, i, dev):
        return copy(SB.at[d, quarter(i)], RB.at[way, d, quarter(i)], cs.at[d, i], cr.at[way, d, i], dev)

    def c_send(way, pos, d, to):
        for i in range(4):
            mine = PF[d, c, quarter(i)] + PR[d, quarter(i)].astype(F32)

            @pl.when(pos == 0)
            def _():
                SB[d, quarter(i)] = mine.astype(BF16)

            @pl.when(pos > 0)
            def _():
                c_copy(way, d, i, {"zl": to}).wait_recv()
                SB[d, quarter(i)] = (mine + RB[way, d, quarter(i)].astype(F32)).astype(BF16)

            c_copy(way, d, i, {"zl": to}).start()

    def c_steps(lo, hi):
        def step(t, carry):
            @pl.when((t >= k) & (k < 7))
            def _():
                c_send(0, k, 7 + k - t, k + 1)

            @pl.when((t >= 7 - k) & (k > 0))
            def _():
                c_send(1, 7 - k, t - 7 + k, k - 1)

            return carry

        lax.fori_loop(lo, hi, step, 0)

    def c_last():
        hg_ref[...] = PF[k, c] + PR[k].astype(F32)

        @pl.when(k > 0)
        def _():
            for i in range(4):
                c_copy(0, k, i, {"zl": k - 1}).wait_recv()
            hg_ref[...] += RB[0, k].astype(F32)

        @pl.when(k < 7)
        def _():
            for i in range(4):
                c_copy(1, k, i, {"zl": k + 1}).wait_recv()
            hg_ref[...] += RB[1, k].astype(F32)


    def dw(q, first=False, last=False):
        zh = lax.rem(zo + q, 4)
        lhs = jnp.concatenate([HT[4 * zh + i] for i in range(4)], axis=1)

        def step(n, carry):
            cols = pl.ds(pl.multiple_of(n * 256, 256), 256)
            rhs = G[zh, :, :, :, cols].reshape(512, 256)
            res = jnp.dot(lhs, rhs, preferred_element_type=F32)
            if last:
                dw_ref[:, cols] = (ACC[:, cols] + res).astype(BF16)
            else:
                ACC[:, cols] = res if first else ACC[:, cols] + res
            return carry

        lax.fori_loop(0, 4, step, 0)

    z_first()
    y_first(0)
    hidden()
    h_first()
    h_last()
    b_first()
    y_relay(0)
    y_last(0)
    x_first(0)
    b_steps(0,1)
    z_relay()
    loads[3].wait()
    terms(0)
    b_steps(1,2)
    z_second()
    y_first(1)
    y_first(3)
    b_steps(2,3)
    y_relay(1)
    y_relay(3)
    z_wait(0,2)
    z_wait(1,2)
    y_first(2)
    y_last(1)
    y_last(3)
    x_first(1)
    x_first(3)
    terms(1,3)
    y_relay(2)
    y_last(2)
    x_first(2)
    terms(2)
    x_relay(0)
    terms_last(0)
    terms_last(1)
    terms_last(3)
    terms_last(2)
    c_steps(0,1)
    c_steps(1,2)
    x_relay(1)
    b_steps(3,4)
    c_steps(2,3)
    x_relay(3)
    b_steps(4,5)
    c_steps(3,4)
    b_steps(5,6)
    c_steps(4,5)
    x_relay(2)
    b_steps(6,7)
    c_steps(5,6)
    b_last()
    x_last(0)
    dw(0,first=True)
    c_steps(6,7)
    x_last(1)
    dw(1)
    x_last(3)
    dw(3)
    c_last()
    x_last(2)
    dw(2,last=True)

    for cp in sends:
        cp.wait_send()

    def drain_b(s, carry):
        for i in range(NB):
            @pl.when((k - s >= 0) & (k < 7))
            def _():
                right(k - s, i, NB * s + i).wait_send()

            @pl.when((k + s <= 7) & (k > 0))
            def _():
                left(k + s, i, NB * s + i).wait_send()

        across(s).wait_send()
        return carry

    lax.fori_loop(0, 8, drain_b, 0)

    def drain_c(d, carry):
        @pl.when(d != k)
        def _():
            for i in range(4):
                c_copy(0, d, i, {"core": 1 - c}).wait_send()

        return carry

    lax.fori_loop(0, 8, drain_c, 0)


def on_device(gate_pre, up_pre, out_grad, down_weight):
    dma = pltpu.SemaphoreType.DMA
    hbm = pl.BlockSpec(memory_space=pltpu.MemorySpace.HBM)
    vmem = pl.BlockSpec(memory_space=pltpu.VMEM)
    act_shape = (32, 1664)
    weight_grad, hidden_grad = pl.pallas_call(
        kernel,
        out_shape=(
            jax.ShapeDtypeStruct((416, 1024), BF16),
            jax.ShapeDtypeStruct(act_shape, F32),
        ),
        in_specs=[hbm] * 4,
        out_specs=(vmem,) * 2,
        scratch_shapes=[
            pltpu.VMEM((4, 4, 4, 32, 1024), BF16),
            pltpu.VMEM((1664, 1024), BF16),
            pltpu.VMEM(act_shape, BF16),
            pltpu.VMEM(act_shape, BF16),
            pltpu.VMEM((4, 32, 512), BF16),
            pltpu.VMEM((4, 32, 512), BF16),
            pltpu.VMEM((16, 416, 128), BF16),
            pltpu.VMEM((8, 2, 32, 1664), F32),
            pltpu.VMEM((8, 2, 32, 1664), BF16),
            pltpu.VMEM((8, 32, 1664), BF16),
            pltpu.VMEM((2, 8, 32, 1664), BF16),
            pltpu.VMEM((8, 32, 1664), BF16),
            pltpu.VMEM((416, 1024), F32),
            dma((4,)),
            dma((2, 3)), dma((2, 3)),
            dma((4, 4)), dma((4, 4)),
            dma((4, 4)), dma((4, 4)),
            dma((3,)), dma((3,)),
            dma((8 * NB,)), dma((8 * NB,)),
            dma((8 * NB,)), dma((8 * NB,)),
            dma((8,)), dma((8,)),
            dma((4,)), dma((4,)),
            dma((8, 4)), dma((2, 8, 4)),
        ],
        compiler_params=pltpu.CompilerParams(
            collective_id=0, has_side_effects=True, vmem_limit_bytes=67043328
        ),
    )(gate_pre, up_pre, out_grad, down_weight)
    gate_vals = gate_pre.astype(F32)
    sigma = jax.nn.sigmoid(gate_vals)
    up_grad = (hidden_grad * (gate_vals * sigma)).astype(BF16)
    slope = up_pre.astype(F32) * sigma * (1.0 + gate_vals * (1.0 - sigma))
    gate_grad = (hidden_grad * slope).astype(BF16)
    return weight_grad, gate_grad, up_grad


def solution(mesh):
    torus = Mesh(mesh.devices.reshape(4, 4, 8, 2, 4), ("zh", "y", "zl", "core", "x"))
    in_specs = (
        P(("zl", "core", "x"), ROW),
        P(("zl", "core", "x"), ROW),
        P(("zh", "y", "x"), COL),
        P(ROW, COL),
    )
    out_specs = (P(("zh", "y", "x"), COL), P(("zl", "core", "x"), ROW), P(("zl", "core", "x"), ROW))
    return jax.shard_map(
        on_device, mesh=torus, in_specs=in_specs, out_specs=out_specs, check_vma=False
    )
```
